256 devices in a mesh: seq: 64 (over z_lo, y, x, core), head: 4 (over z_hi).
Axes of the slice: x: 4, y: 4, z: 8 (z_hi: 4, z_lo: 2; z = z_hi * 2 + z_lo), core: 2. Of those that a mesh axis runs over, the one named last changes fastest.
Arguments:
- queries: bfloat16 [8192, 4096], P('seq', 'head'), may hold values from -500 to 500
- first_key_rows: bfloat16 [8192, 2048], P('seq', 'head'), may hold values from -6 to 6
- first_value_rows: bfloat16 [8192, 2048], P('seq', 'head'), may hold values from -6 to 6
- second_key_rows: bfloat16 [8192, 2048], P('seq', 'head'), may hold values from -6 to 6
- second_value_rows: bfloat16 [8192, 2048], P('seq', 'head'), may hold values from -6 to 6
- out_weight: bfloat16 [4096, 4096], P('head'), may hold values from -6 to 6
Outputs:
- projected: bfloat16 [8192, 4096], P('seq', 'head')
The draws below stay inside these ranges and needn't reach their ends.
All inputs are finite; a program needn't handle non-finite values.
Results may differ from the reference program's by a relative error of at most 0.015.
The reference program's roundings to bfloat16 on the way count: a program that leaves them out, or rounds other values in their place, can miss the bound.
Values may be sent and summed in bfloat16 or wider, within the bound.
No kernel may reach another device: no remote copies, remote signals or barrier semaphores. Data moves between devices by JAX's collectives and lax.ppermute only.
A program may use at most 64 MiB of HBM per device.

```python
import jax
import jax.numpy as jnp
from jax import lax

D = 4096
QUERY_HEADS = 32
KEY_VALUE_HEADS = 16
HEAD_SIZE = 128
W1 = 512
W2 = 32
R = 128
TOTAL_TOKENS = 8192
N_HEAD = 4


def draw_queries(key, part):
    key_base = jax.random.fold_in(key, 0)
    values_drawn = jnp.clip(jax.random.normal(key_base, (TOTAL_TOKENS, QUERY_HEADS * HEAD_SIZE), jnp.float32), -6.0, 6.0)
    return values_drawn.astype(jnp.bfloat16)


def level_of(rng, shape, cuts, least, high):
    gain, own = 1.0, jax.random.fold_in(rng, 6)
    for dim, blocks in cuts:
        heights = jnp.exp(jax.random.uniform(jax.random.fold_in(own, dim), (blocks,), jnp.float32, least / len(cuts), high / len(cuts)))
        gain = gain * jnp.repeat(heights, shape[dim] // blocks).reshape([-1 if axis == dim else 1 for axis in range(len(shape))])
    return gain


def gaussian(rng, shape, deviation, most, pieces=(), held_as=jnp.bfloat16):
    result = deviation * jax.random.normal(rng, shape, jnp.float32)
    if pieces:
        result = result * level_of(rng, shape, pieces, -0.22, 0.18)
    return jnp.clip(result, -most, most).astype(held_as)


def setup_inputs(seed: int = 0) -> dict:
    key_of = jax.random.split(jax.random.key(seed), 7)
    return {
        "queries": draw_queries(jax.random.fold_in(key_of[6], 71), 0),
        "first_key_rows": gaussian(key_of[1], (TOTAL_TOKENS, KEY_VALUE_HEADS * HEAD_SIZE), 1.0, 6.0, ((0, 64), (1, 4))),
        "first_value_rows": gaussian(key_of[2], (TOTAL_TOKENS, KEY_VALUE_HEADS * HEAD_SIZE), 1.0, 6.0, ((0, 64), (1, 4))),
        "second_key_rows": gaussian(key_of[3], (TOTAL_TOKENS, KEY_VALUE_HEADS * HEAD_SIZE), 1.0, 6.0, ((0, 64), (1, 4))),
        "second_value_rows": gaussian(key_of[4], (TOTAL_TOKENS, KEY_VALUE_HEADS * HEAD_SIZE), 1.0, 6.0, ((0, 64), (1, 4))),
        "out_weight": gaussian(key_of[5], (QUERY_HEADS * HEAD_SIZE, D), 1.0, 6.0, ((0, 4),)),
    }


def window_attend(query_block, outer_keys, outer_values, inner_keys, inner_values, first_pos):
    row_count = query_block.shape[0]
    inner_span = inner_keys.shape[0] - row_count
    outer_span = outer_keys.shape[0] - row_count
    scale_factor = query_block.shape[1] ** -0.5
    inner_key_win = jnp.stack([inner_keys[inner_span - offset:inner_span - offset + row_count] for offset in range(inner_span)])
    inner_val_win = jnp.stack([inner_values[inner_span - offset:inner_span - offset + row_count] for offset in range(inner_span)])
    blended = (query_block.astype(jnp.float32)[None] * inner_key_win.astype(jnp.float32)).astype(jnp.bfloat16)
    scores = jnp.einsum("wid,jd->wij", blended.astype(jnp.float32), outer_keys.astype(jnp.float32)) * scale_factor
    row_index = lax.broadcasted_iota(jnp.int32, scores.shape, 1)
    col_index = lax.broadcasted_iota(jnp.int32, scores.shape, 2)
    lag_index = lax.broadcasted_iota(jnp.int32, scores.shape, 0)
    allowed = (col_index > row_index) & (col_index <= row_index + outer_span)
    allowed = allowed & (first_pos - outer_span + col_index >= 0) & (first_pos + row_index - lag_index >= 0)
    scores = jnp.where(allowed, scores, -1e30)
    row_max = jnp.max(scores, axis=(0, 2), keepdims=True)
    expon = jnp.where(allowed, jnp.exp(scores - row_max), 0.0)
    row_total = jnp.sum(expon, axis=(0, 2), keepdims=True)
    weights = (expon / row_total).astype(jnp.bfloat16)
    inner_sum = jnp.einsum("wij,jd->wid", weights.astype(jnp.float32), outer_values.astype(jnp.float32))
    return jnp.sum(inner_val_win.astype(jnp.float32) * inner_sum, axis=0)


def reference(queries, first_key_rows, first_value_rows, second_key_rows, second_value_rows, out_weight):
    token_count = queries.shape[0]
    query_group_width = QUERY_HEADS // KEY_VALUE_HEADS
    block_count = token_count // R
    outer_keys_pad = jnp.pad(first_key_rows, ((W1, 0), (0, 0)))
    outer_vals_pad = jnp.pad(first_value_rows, ((W1, 0), (0, 0)))
    inner_keys_pad = jnp.pad(second_key_rows, ((W2, 0), (0, 0)))
    inner_vals_pad = jnp.pad(second_value_rows, ((W2, 0), (0, 0)))

    def per_head(head):
        kv_start = (head // query_group_width) * HEAD_SIZE
        query_cols = lax.dynamic_slice_in_dim(queries, head * HEAD_SIZE, HEAD_SIZE, 1)
        key_one = lax.dynamic_slice_in_dim(outer_keys_pad, kv_start, HEAD_SIZE, 1)
        val_one = lax.dynamic_slice_in_dim(outer_vals_pad, kv_start, HEAD_SIZE, 1)
        key_two = lax.dynamic_slice_in_dim(inner_keys_pad, kv_start, HEAD_SIZE, 1)
        val_two = lax.dynamic_slice_in_dim(inner_vals_pad, kv_start, HEAD_SIZE, 1)

        def per_block(block):
            first_pos = block * R
            return window_attend(
                lax.dynamic_slice_in_dim(query_cols, first_pos, R, 0),
                lax.dynamic_slice_in_dim(key_one, first_pos, W1 + R, 0),
                lax.dynamic_slice_in_dim(val_one, first_pos, W1 + R, 0),
                lax.dynamic_slice_in_dim(key_two, first_pos, W2 + R, 0),
                lax.dynamic_slice_in_dim(val_two, first_pos, W2 + R, 0),
                first_pos).astype(jnp.bfloat16)

        return lax.map(per_block, jnp.arange(block_count, dtype=jnp.int32)).reshape(token_count, HEAD_SIZE)

    heads_out = lax.map(per_head, jnp.arange(QUERY_HEADS, dtype=jnp.int32))
    attended = jnp.transpose(heads_out, (1, 0, 2)).reshape(token_count, QUERY_HEADS * HEAD_SIZE)
    group_rows = QUERY_HEADS * HEAD_SIZE // N_HEAD
    summed = jnp.zeros((token_count, D), jnp.float32)
    for group in range(N_HEAD):
        part_term = jnp.dot(attended[:, group * group_rows:(group + 1) * group_rows],
                            out_weight[group * group_rows:(group + 1) * group_rows],
                            preferred_element_type=jnp.float32)
        summed = summed + lax.optimization_barrier(part_term.astype(jnp.bfloat16)).astype(jnp.float32)
    return summed.astype(jnp.bfloat16)
```

```python
import math

import jax
import jax.numpy as jnp
from jax import lax
from jax.experimental import pallas as pl
from jax.experimental.pallas import tpu as pltpu
from jax.sharding import PartitionSpec as P

HS = 128
W1 = 512
W2 = 32
R = 128
L = 8
M = L * R
NCH = W2 // L
KEYS = W1 + R
C = math.log2(math.e) / math.sqrt(HS)
BIG = 1e30
F32 = jnp.float32
BF16 = jnp.bfloat16


def attn_body(
    sh_ref, q_ref, ko, vo, kx0, vx0, kp2, vp2, kx2, vx2, kp4, vp4, kx4, vx4,
    k2o, v2o, k2t, v2t, o_ref,
    ks, vs, k2f, v2f, pen, a0, a1, s0, s1, p0, p1, r0, r1, m_ref, l_ref, acc,
):
    g = pl.program_id(0)
    sh = sh_ref[0]
    even = lax.rem(sh, 2) == 0
    row = lax.broadcasted_iota(jnp.int32, (R, HS), 0)
    col = lax.broadcasted_iota(jnp.int32, (R, HS), 1)
    up = col > row
    upb = jnp.where(up, 1.0, 0.0).astype(BF16)
    tp = [jnp.where(sh - 4 + t < 0, BIG, 0.0).astype(F32) for t in range(4)]

    @pl.when(g == 0)
    def _():
        base = jnp.where(up, tp[0], 0.0)
        for w in range(W2):
            pen[pl.ds(w * R, R), :] = jnp.where((row < w) & (sh == 0), BIG, base)

    for dst, p4, x4, p2, x2, x0, own in (
        (ks, kp4, kx4, kp2, kx2, kx0, ko),
        (vs, vp4, vx4, vp2, vx2, vx0, vo),
    ):
        dst[0:128, :] = p4[...]
        dst[256:384, :] = p2[...]
        dst[512:640, :] = own[...]

        @pl.when(even)
        def _():
            dst[128:256, :] = x4[...]
            dst[384:512, :] = x2[...]

        @pl.when(jnp.logical_not(even))
        def _():
            dst[128:256, :] = x2[...]
            dst[384:512, :] = x0[...]

    k2f[0:W2, :] = k2t[...].astype(F32)
    k2f[W2:, :] = k2o[...].astype(F32)
    v2f[0:W2, :] = v2t[...].astype(F32)
    v2f[W2:, :] = v2o[...].astype(F32)
    A, S, Pm, Rr = [a0, a1], [s0, s1], [p0, p1], [r0, r1]
    units = [(hh, c) for hh in range(2) for c in range(NCH)]

    def qk(u):
        hh, c = units[u]
        a, s = A[u % 2], S[u % 2]
        qf = q_ref[:, hh * HS : (hh + 1) * HS].astype(F32)
        for x in range(L):
            w = c * L + x
            a[x * R : (x + 1) * R, :] = (qf * k2f[W2 - w : W2 - w + R, :]).astype(BF16)
        s[...] = lax.dot_general(
            a[...], ks[...], (((1,), (1,)), ((), ())), preferred_element_type=F32
        )

    def soft(u):
        hh, c = units[u]
        s, p = S[u % 2], Pm[u % 2]
        mt = [None] * 4
        for x in range(L):
            w = c * L + x
            rs = slice(x * R, (x + 1) * R)
            sm = jnp.where(up, s[rs, 0:128], s[rs, 512:640]) - pen[w * R : (w + 1) * R, :]
            s[rs, 0:128] = sm
            mt[0] = sm if x == 0 else jnp.maximum(mt[0], sm)
            for t in range(1, 4):
                b = s[rs, t * 128 : (t + 1) * 128]
                mt[t] = b if x == 0 else jnp.maximum(mt[t], b)
        mx = mt[0]
        for t in range(1, 4):
            mx = jnp.maximum(mx, mt[t] - tp[t])
        mrow = jnp.max(mx, axis=1, keepdims=True)
        if c == 0:
            mnew, al = jnp.broadcast_to(mrow, (R, HS)), None
        else:
            mold = m_ref[...]
            mnew = jnp.maximum(mold, mrow)
            al = jnp.exp2((mold - mnew) * C)
        m_ref[...] = mnew
        mc = mnew * C
        ls = None
        for x in range(L):
            rs = slice(x * R, (x + 1) * R)
            for t in range(4):
                sub = mc if t == 0 else mc + tp[t]
                e = jnp.exp2(s[rs, t * 128 : (t + 1) * 128] * C - sub)
                ls = e if ls is None else ls + e
                eb = e.astype(BF16)
                if t == 0:
                    e0 = eb * upb
                    p[rs, 0:128] = e0
                    p[rs, 512:640] = eb - e0
                else:
                    p[rs, t * 128 : (t + 1) * 128] = eb
        l_ref[...] = ls if c == 0 else l_ref[...] * al + ls
        return al

    def pv(u, al):
        hh, c = units[u]
        p, r = Pm[u % 2], Rr[u % 2]
        r[...] = lax.dot_general(
            p[...], vs[...], (((1,), (0,)), ((), ())), preferred_element_type=F32
        )
        o = None
        for x in range(L):
            w = c * L + x
            t = v2f[W2 - w : W2 - w + R, :] * r[x * R : (x + 1) * R, :]
            o = t if o is None else o + t
        if c > 0:
            o = acc[...] * al + o
        if c < NCH - 1:
            acc[...] = o
        else:
            total = jnp.sum(l_ref[...], axis=1, keepdims=True)
            o_ref[:, hh * HS : (hh + 1) * HS] = (o / total).astype(BF16)

    qk(0)
    for u in range(len(units)):
        if u + 1 < len(units):
            qk(u + 1)
        pv(u, soft(u))


def attend(shard, q, kv, x0, p2, x2, p4, x4, k2, v2, tail):
    groups = kv.shape[1] // HS
    kblock = pl.BlockSpec((R, HS), lambda g: (0, g))
    vblock = pl.BlockSpec((R, HS), lambda g: (1, g))
    pairs = []
    for piece in (kv, x0, p2, x2, p4, x4):
        pairs += [piece, piece]
    return pl.pallas_call(
        attn_body,
        out_shape=jax.ShapeDtypeStruct(q.shape, BF16),
        grid=(groups,),
        in_specs=[
            pl.BlockSpec(memory_space=pltpu.SMEM),
            pl.BlockSpec((R, 2 * HS), lambda g: (0, g)),
        ]
        + [kblock, vblock] * 6
        + [
            kblock,
            kblock,
            pl.BlockSpec((W2, HS), lambda g: (0, g)),
            pl.BlockSpec((W2, HS), lambda g: (1, g)),
        ],
        out_specs=pl.BlockSpec((R, 2 * HS), lambda g: (0, g)),
        scratch_shapes=[pltpu.VMEM((KEYS, HS), BF16)] * 2
        + [pltpu.VMEM((W2 + R, HS), F32)] * 2
        + [pltpu.VMEM((W2 * R, HS), F32)]
        + [pltpu.VMEM((M, HS), BF16)] * 2
        + [pltpu.VMEM((M, KEYS), F32)] * 2
        + [pltpu.VMEM((M, KEYS), BF16)] * 2
        + [pltpu.VMEM((M, HS), F32)] * 2
        + [pltpu.VMEM((R, HS), F32)] * 3,
        compiler_params=pltpu.CompilerParams(vmem_limit_bytes=24 * 2**20),
        cost_estimate=pl.CostEstimate(
            flops=4 * W2 * R * KEYS * HS * 2 * groups,
            bytes_accessed=3 * 2**20,
            transcendentals=W2 * R * W1 * 2 * groups,
        ),
        name="attn",
    )(shard, q, *pairs, k2, v2, tail, tail)


def proj_body(i_ref, a_ref, w_ref, o_ref):
    o_ref[...] = lax.dot_general(
        a_ref[...], w_ref[...], (((1,), (0,)), ((), ())), preferred_element_type=F32
    ).astype(BF16)


def project(block, attended, weight):
    rows, depth = attended.shape
    width = weight.shape[1] // 4
    tile = 256
    return pl.pallas_call(
        proj_body,
        out_shape=jax.ShapeDtypeStruct((rows, width), BF16),
        grid_spec=pltpu.PrefetchScalarGridSpec(
            num_scalar_prefetch=1,
            grid=(width // tile,),
            in_specs=[
                pl.BlockSpec((rows, depth), lambda j, i: (0, 0)),
                pl.BlockSpec((depth, tile), lambda j, i: (0, i[0] * (width // tile) + j)),
            ],
            out_specs=pl.BlockSpec((rows, tile), lambda j, i: (0, j)),
        ),
        cost_estimate=pl.CostEstimate(
            flops=2 * rows * depth * width, bytes_accessed=2 * depth * width, transcendentals=0
        ),
        name="proj",
    )(block, attended, weight)


def local(queries, first_key_rows, first_value_rows, second_key_rows, second_value_rows, out_weight):
    seq = lax.axis_size("seq")
    shard = lax.axis_index("seq").astype(jnp.int32).reshape(1)
    me = lax.axis_index("head").astype(jnp.int32)

    def behind(x, by):
        return lax.ppermute(x, "seq", [(i, (i + by) % seq) for i in range(seq)])

    def swap(x):
        return lax.ppermute(x, "seq", [(i, i ^ 1) for i in range(seq)])

    kv = jnp.concatenate([first_key_rows, first_value_rows], axis=0)
    tail = jnp.concatenate([second_key_rows[R - W2 :], second_value_rows[R - W2 :]], axis=0)
    p2 = behind(kv, 2)
    p4 = behind(kv, 4)
    t1 = behind(tail, 1)
    x0 = swap(kv)
    x2 = swap(p2)
    x4 = swap(p4)
    attended = attend(
        shard, queries, kv, x0, p2, x2, p4, x4, second_key_rows, second_value_rows, t1
    )
    got = []
    for d in (2, 1, 3):
        piece = project(lax.rem(me + d, 4).reshape(1), attended, out_weight)
        got.append(lax.ppermute(piece, "head", [(i, (i + d) % 4) for i in range(4)]))
    total = project(me.reshape(1), attended, out_weight).astype(F32)
    for piece in got:
        total = total + piece.astype(F32)
    return total.astype(BF16)


def solution(mesh):
    in_specs = (P("seq", "head"),) * 5 + (P("head", None),)
    return jax.shard_map(
        local, mesh=mesh, in_specs=in_specs, out_specs=P("seq", "head"), check_vma=False
    )
```

```python
import math

import jax
import jax.numpy as jnp
from jax import lax
from jax.experimental import pallas as pl
from jax.experimental.pallas import tpu as pltpu
from jax.sharding import PartitionSpec as P

HS = 128
W1 = 512
W2 = 32
R = 128
IB = 32
LANES = W2 * IB
KEYS = W1 + R
NT = 512
KS = LANES // NT
LT = NT // 128
CH = 16
CHAIN = False
C = math.log2(math.e) / math.sqrt(HS)
BIG = 1e30
F32 = jnp.float32
BF16 = jnp.bfloat16
PARAMS = pltpu.CompilerParams(vmem_limit_bytes=60 * 2**20)


def attn_body(blocks, *refs):
    refs = list(refs)
    sh_ref, q_ref, k2o, k2t, v2o, v2t = (refs.pop(0) for _ in range(6))
    pieces = [(refs.pop(0), refs.pop(0)) for _ in range(6)]
    w_hbm = refs.pop(0)
    outs = [refs.pop(0) for _ in range(4)]
    ks, vt, k2f, v2f, w2t, penA, penB, a0, a1, s0, s1, p0, p1, m_ref, att, wbuf, wsem = refs
    g, last = pl.program_id(0), pl.num_programs(0) - 1
    depth = w_hbm.shape[0] // 4

    def fetch(i):
        rows = slice(i * depth, (i + 1) * depth)
        return pltpu.make_async_copy(w_hbm.at[rows, :], wbuf.at[rows, :], wsem.at[i])

    @pl.when(g == 0)
    def _():
        for i in range(4):
            fetch(i).start()

    sh, me = sh_ref[0], sh_ref[1]
    tp = [jnp.where(sh - 4 + t < 0, BIG, 0.0).astype(F32) for t in range(4)]

    def put(tile, piece):
        rows = slice(tile * R, (tile + 1) * R)
        ks[rows, :] = piece[0][...]
        vt[0:HS, rows] = piece[1][...].T

    own, x0, p2, x2, p4, x4 = pieces
    even = lax.rem(sh, 2) == 0
    put(0, p4)
    put(2, p2)

    @pl.when(even)
    def _():
        put(1, x4)
        put(3, x2)

    @pl.when(jnp.logical_not(even))
    def _():
        put(1, x2)
        put(3, x0)

    put(4, own)

    @pl.when(pl.program_id(0) == 0)
    def _():
        vt[HS:, :] = jnp.ones((16, KEYS), BF16)
        r = lax.broadcasted_iota(jnp.int32, (IB, LANES), 0)
        lane = lax.broadcasted_iota(jnp.int32, (IB, LANES), 1)
        ii, w = lax.rem(lane, IB), lax.div(lane, IB)
        penA[...] = jnp.where(r > ii, tp[0], BIG)
        penB[0] = jnp.where((r > ii) | ((sh == 0) & (w > ii)), BIG, 0.0)
        penB[1] = jnp.where(r > ii, BIG, 0.0)

    k2f[0:W2, :] = k2t[...].astype(F32)
    k2f[W2:, :] = k2o[...].astype(F32)
    v2f[0:W2, :] = v2t[...].astype(F32)
    v2f[W2:, :] = v2o[...].astype(F32)
    for x, b in enumerate(blocks):
        for w in range(0, W2, 4):
            at = W2 + IB * b - w
            blk = jnp.concatenate([v2f[at - y : at - y + IB, :] for y in range(4)], 0)
            w2t[x, :, w * IB : (w + 4) * IB] = blk.T

    A, S, Pm = [a0, a1], [s0, s1], [p0, p1]
    units = [(hh, x) for hh in range(2) for x in range(len(blocks))]
    n = W1 + IB

    def pen(b, r, k):
        cols = slice(k * NT, (k + 1) * NT)
        if r < IB:
            return penA[r : r + 8, cols]
        if r >= W1:
            return penB[0 if b == 0 else 1, r - W1 : r - W1 + 8, cols]
        return None

    def qk(u, k):
        hh, b = units[u][0], blocks[units[u][1]]
        a, s, lo = A[u % 2], S[u % 2], IB * b
        qf = q_ref[lo : lo + IB, hh * HS : (hh + 1) * HS].astype(F32)
        cols = slice(k * NT, (k + 1) * NT)
        for w in range(k * NT // IB, (k + 1) * NT // IB):
            at = W2 + lo - w
            a[w * IB : (w + 1) * IB, :] = (qf * k2f[at : at + IB, :]).astype(BF16)
        x = lax.dot_general(
            ks[lo : lo + n, :], a[cols, :], (((1,), (1,)), ((), ())), preferred_element_type=F32
        )
        s[:, cols] = x
        top = {}
        for r in range(0, n, 8):
            y, pe = x[r : r + 8, :], pen(b, r, k)
            key = "m" if pe is not None else (lo + r) // R
            if pe is not None:
                y = y - pe
            top[key] = y if key not in top else jnp.maximum(top[key], y)
        m8 = None
        for key, y in top.items():
            if key != "m" and key != 4:
                y = y - tp[key]
            for t in range(LT):
                z = y[:, t * 128 : (t + 1) * 128]
                m8 = z if m8 is None else jnp.maximum(m8, z)
        return m8

    def qk_all(u):
        m8 = qk(u, 0)
        for k in range(1, KS):
            m8 = jnp.maximum(m8, qk(u, k))
        m1 = jnp.max(m8, axis=0, keepdims=True)
        m1 = jnp.maximum(m1, pltpu.roll(m1, 32, 1))
        m1 = jnp.maximum(m1, pltpu.roll(m1, 64, 1))
        m_ref[u % 2] = jnp.broadcast_to(m1 * C, (8, HS))

    def ex(u, k):
        b = blocks[units[u][1]]
        s, p, lo = S[u % 2], Pm[u % 2], IB * b
        cols = slice(k * NT, (k + 1) * NT)
        mb = jnp.concatenate([m_ref[u % 2]] * LT, axis=1)
        for r in range(0, n, CH):
            es = []
            for r8 in range(r, r + CH, 8):
                pe, t = pen(b, r8, k), (lo + r8) // R
                sub = mb + pe if pe is not None else (mb + tp[t] if t < 4 else mb)
                es.append(jnp.exp2(s[r8 : r8 + 8, cols] * C - sub))
            p[r : r + CH, cols] = jnp.concatenate(es, 0).astype(BF16)

    def pv_all(u):
        hh, x = units[u]
        lo, p = IB * blocks[x], Pm[u % 2]
        o = l = None
        for k in range(KS):
            cols = slice(k * NT, (k + 1) * NT)
            rt = lax.dot_general(
                vt[:, lo : lo + n], p[:, cols], (((1,), (0,)), ((), ())), preferred_element_type=F32
            )
            for t in range(LT):
                part = slice(t * 128, (t + 1) * 128)
                y = rt[0:HS, part] * w2t[x, :, k * NT + t * 128 : k * NT + (t + 1) * 128]
                z = rt[HS : HS + 8, part]
                o, l = (y, z) if o is None else (o + y, l + z)
        l = l[0:1, :]
        l = l + pltpu.roll(l, 32, 1)
        l = l + pltpu.roll(l, 64, 1)
        o = o + pltpu.roll(o, 32, 1)
        o = o + pltpu.roll(o, 64, 1)
        o = (o / l).T
        start = pl.multiple_of((2 * g + hh) * HS, HS)
        att[IB * x : IB * (x + 1), pl.ds(start, HS)] = o[0:IB, :].astype(BF16)

    for t in range(-1, len(units) + 1):

        @pl.when(sh >= 0)
        def _():
            if t + 1 < len(units):
                qk_all(t + 1)
            if 0 <= t < len(units):
                for k in range(KS):
                    ex(t, k)
            if t >= 1:
                pv_all(t - 1)

    @pl.when(g == last)
    def _():
        for i in range(4):
            fetch(i).wait()
        width = outs[0].shape[1]
        for d, out in enumerate(outs):
            start = pl.multiple_of(lax.rem(me + d, 4) * width, width)
            out[...] = lax.dot_general(
                att[...], wbuf[:, pl.ds(start, width)], (((1,), (0,)), ((), ())),
                preferred_element_type=F32,
            ).astype(BF16)


def attend(where, q, k2, v2, tail, pieces, weight):
    groups = k2.shape[1] // HS
    width = weight.shape[1] // 4
    nb = R // IB
    kblock = pl.BlockSpec((R, HS), lambda g: (0, g))
    vblock = pl.BlockSpec((R, HS), lambda g: (1, g))
    args = []
    for piece in pieces:
        args += [piece, piece]
    return pl.pallas_call(
        lambda *refs: attn_body(tuple(range(nb)), *refs),
        out_shape=(jax.ShapeDtypeStruct((R, width), BF16),) * 4,
        grid=(groups,),
        in_specs=[
            pl.BlockSpec(memory_space=pltpu.SMEM),
            pl.BlockSpec((R, 2 * HS), lambda g: (0, g)),
            kblock,
            pl.BlockSpec((W2, HS), lambda g: (0, g)),
            kblock,
            pl.BlockSpec((W2, HS), lambda g: (1, g)),
        ]
        + [kblock, vblock] * len(pieces)
        + [pl.BlockSpec(memory_space=pl.ANY)],
        out_specs=(pl.BlockSpec((R, width), lambda g: (0, 0)),) * 4,
        scratch_shapes=[pltpu.VMEM((KEYS, HS), BF16), pltpu.VMEM((HS + 16, KEYS), BF16)]
        + [pltpu.VMEM((W2 + R, HS), F32)] * 2
        + [pltpu.VMEM((nb, HS, LANES), F32)]
        + [pltpu.VMEM((IB, LANES), F32), pltpu.VMEM((2, IB, LANES), F32)]
        + [pltpu.VMEM((LANES, HS), BF16)] * 2
        + [pltpu.VMEM((W1 + IB, LANES), F32)] * 2
        + [pltpu.VMEM((W1 + IB, LANES), BF16)] * 2
        + [pltpu.VMEM((2, 8, HS), F32), pltpu.VMEM(q.shape, BF16)]
        + [pltpu.VMEM(weight.shape, BF16), pltpu.SemaphoreType.DMA((4,))],
        compiler_params=PARAMS,
        cost_estimate=pl.CostEstimate(
            flops=4 * W2 * R * KEYS * HS * 2 * groups * 4,
            bytes_accessed=12 * 2**20,
            transcendentals=W2 * R * W1 * 2 * groups,
        ),
        name="attn",
    )(where, q, k2, tail, v2, tail, *args, weight)


def pack_body(k_ref, v_ref, k2_ref, v2_ref, kv_ref, t_ref):
    kv_ref[0:R, :] = k_ref[...]
    kv_ref[R:, :] = v_ref[...]
    t_ref[0:W2, :] = k2_ref[...]
    t_ref[W2:, :] = v2_ref[...]


def pack(k, v, k2, v2):
    width, cols = k.shape[1], 2 * HS
    block = pl.BlockSpec((R, cols), lambda i: (0, i))
    last = pl.BlockSpec((W2, cols), lambda i: (R // W2 - 1, i))
    return pl.pallas_call(
        pack_body,
        out_shape=(
            jax.ShapeDtypeStruct((2 * R, width), BF16),
            jax.ShapeDtypeStruct((2 * W2, width), BF16),
        ),
        grid=(width // cols,),
        in_specs=[block, block, last, last],
        out_specs=(
            pl.BlockSpec((2 * R, cols), lambda i: (0, i)),
            pl.BlockSpec((2 * W2, cols), lambda i: (0, i)),
        ),
        compiler_params=PARAMS,
        name="pack",
    )(k, v, k2, v2)


def add_body(*refs):
    x = [r[...].astype(F32) for r in refs[:-1]]
    refs[-1][...] = (x[0] + x[1] + x[2] + x[3]).astype(BF16)


def local(queries, first_key_rows, first_value_rows, second_key_rows, second_value_rows, out_weight):
    seq = lax.axis_size("seq")
    where = jnp.stack([lax.axis_index("seq"), lax.axis_index("head")]).astype(jnp.int32)

    def behind(x, by):
        return lax.ppermute(x, "seq", [(i, (i + by) % seq) for i in range(seq)])

    def swap(x):
        return lax.ppermute(x, "seq", [(i, i ^ 1) for i in range(seq)])

    kv, tail = pack(first_key_rows, first_value_rows, second_key_rows, second_value_rows)
    p2 = behind(kv, 2)
    p4 = behind(p2, 2) if CHAIN else behind(kv, 4)
    x0 = swap(kv)
    t1 = behind(tail, 1)
    x2 = swap(p2)
    x4 = swap(p4)
    pieces = attend(
        where, queries, second_key_rows, second_value_rows, t1, (kv, x0, p2, x2, p4, x4), out_weight
    )
    got = [pieces[0]]
    for d in (2, 1, 3):
        got.append(lax.ppermute(pieces[d], "head", [(i, (i + d) % 4) for i in range(4)]))
    cols = queries.shape[1] // 2
    block = pl.BlockSpec((R, cols), lambda i: (0, i))
    return pl.pallas_call(
        add_body,
        out_shape=jax.ShapeDtypeStruct(queries.shape, BF16),
        grid=(2,),
        in_specs=[block] * 4,
        out_specs=block,
        compiler_params=PARAMS,
        name="add",
    )(*got)


def solution(mesh):
    in_specs = (P("seq", "head"),) * 5 + (P("head", None),)
    return jax.shard_map(
        local, mesh=mesh, in_specs=in_specs, out_specs=P("seq", "head"), check_vma=False
    )
```

```python
import math

import jax
import jax.numpy as jnp
from jax import lax
from jax.experimental import pallas as pl
from jax.experimental.pallas import tpu as pltpu
from jax.sharding import PartitionSpec as P


HS = 128
W1 = 512
W2 = 32
R = 128
IB = 32
LANES = W2 * IB
KEYS = W1 + R
NT = 512
KS = LANES // NT
LT = NT // 128
CH = 16
C = math.log2(math.e) / math.sqrt(HS)
BIG = 1e30
F32 = jnp.float32
BF16 = jnp.bfloat16
PARAMS = pltpu.CompilerParams(vmem_limit_bytes=46 * 2**20)
SMALL = pltpu.CompilerParams(vmem_limit_bytes=8 * 2**20)


def attn_body(blocks, final, *refs):
    refs = list(refs)
    sh_ref, me_ref, q_ref, k2o, v2o = (refs.pop(0) for _ in range(5))
    tails = [(refs.pop(0), refs.pop(0)) for _ in range(2)]
    pieces = [(refs.pop(0), refs.pop(0)) for _ in range(6)]
    g, last = pl.program_id(0), pl.num_programs(0) - 1
    if final:
        done_ref, w_hbm = refs.pop(0), refs.pop(0)
        outs = [refs.pop(0) for _ in range(4)]
        att, wbuf, wsem = refs[-3:]
        refs = refs[:-3]
        depth = w_hbm.shape[0] // 4

        def fetch(i):
            rows = slice(i * depth, (i + 1) * depth)
            return pltpu.make_async_copy(w_hbm.at[rows, :], wbuf.at[rows, :], wsem.at[i])

        @pl.when(g == 0)
        def _():
            for i in range(4):
                fetch(i).start()
            att[:, 0 : done_ref.shape[1]] = done_ref[...]

    else:
        o_ref = refs.pop(0)
    ks, vt, k2f, v2f, w2t, penA, penB, a0, a1, s0, s1, p0, p1, m_ref = refs

    sh, me = sh_ref[0], me_ref[0]
    tp = [jnp.where(sh - 4 + t < 0, BIG, 0.0).astype(F32) for t in range(4)]

    def put(tile, piece):
        rows = slice(tile * R, (tile + 1) * R)
        ks[rows, :] = piece[0][...]
        vt[0:HS, rows] = piece[1][...].T

    own, x0, p2, x2, p4, x4 = pieces
    even = lax.rem(sh, 2) == 0
    put(0, p4)
    put(2, p2)

    @pl.when(even)
    def _():
        put(1, x4)
        put(3, x2)
        k2f[0:W2, :] = tails[1][0][...].astype(F32)
        v2f[0:W2, :] = tails[1][1][...].astype(F32)

    @pl.when(jnp.logical_not(even))
    def _():
        put(1, x2)
        put(3, x0)
        k2f[0:W2, :] = tails[0][0][...].astype(F32)
        v2f[0:W2, :] = tails[0][1][...].astype(F32)

    put(4, own)

    @pl.when(pl.program_id(0) == 0)
    def _():
        vt[HS:, :] = jnp.ones((16, KEYS), BF16)
        r = lax.broadcasted_iota(jnp.int32, (IB, LANES), 0)
        lane = lax.broadcasted_iota(jnp.int32, (IB, LANES), 1)
        ii, w = lax.rem(lane, IB), lax.div(lane, IB)
        penA[...] = jnp.where(r > ii, tp[0], BIG)
        penB[0] = jnp.where((r > ii) | ((sh == 0) & (w > ii)), BIG, 0.0)
        penB[1] = jnp.where(r > ii, BIG, 0.0)

    k2f[W2:, :] = k2o[...].astype(F32)
    v2f[W2:, :] = v2o[...].astype(F32)
    for x, b in enumerate(blocks):
        for w in range(0, W2, 4):
            at = W2 + IB * b - w
            blk = jnp.concatenate([v2f[at - y : at - y + IB, :] for y in range(4)], 0)
            w2t[x, :, w * IB : (w + 4) * IB] = blk.T

    A, S, Pm = [a0, a1], [s0, s1], [p0, p1]
    units = [(hh, x) for hh in range(2) for x in range(len(blocks))]
    n = W1 + IB

    def pen(b, r, k):
        cols = slice(k * NT, (k + 1) * NT)
        if r < IB:
            return penA[r : r + 8, cols]
        if r >= W1:
            return penB[0 if b == 0 else 1, r - W1 : r - W1 + 8, cols]
        return None

    def qk(u, k):
        hh, b = units[u][0], blocks[units[u][1]]
        a, s, lo = A[u % 2], S[u % 2], IB * b
        qf = q_ref[lo : lo + IB, hh * HS : (hh + 1) * HS].astype(F32)
        cols = slice(k * NT, (k + 1) * NT)
        for w in range(k * NT // IB, (k + 1) * NT // IB):
            at = W2 + lo - w
            a[w * IB : (w + 1) * IB, :] = (qf * k2f[at : at + IB, :]).astype(BF16)
        x = lax.dot_general(
            ks[lo : lo + n, :], a[cols, :], (((1,), (1,)), ((), ())), preferred_element_type=F32
        )
        s[:, cols] = x
        top = {}
        for r in range(0, n, 8):
            y, pe = x[r : r + 8, :], pen(b, r, k)
            key = "m" if pe is not None else (lo + r) // R
            if pe is not None:
                y = y - pe
            top[key] = y if key not in top else jnp.maximum(top[key], y)
        m8 = None
        for key, y in top.items():
            if key != "m" and key != 4:
                y = y - tp[key]
            for t in range(LT):
                z = y[:, t * 128 : (t + 1) * 128]
                m8 = z if m8 is None else jnp.maximum(m8, z)
        return m8

    def qk_all(u):
        m8 = qk(u, 0)
        for k in range(1, KS):
            m8 = jnp.maximum(m8, qk(u, k))
        m1 = jnp.max(m8, axis=0, keepdims=True)
        m1 = jnp.maximum(m1, pltpu.roll(m1, 32, 1))
        m1 = jnp.maximum(m1, pltpu.roll(m1, 64, 1))
        m_ref[u % 2] = jnp.broadcast_to(m1 * C, (8, HS))

    def ex(u, k):
        b = blocks[units[u][1]]
        s, p, lo = S[u % 2], Pm[u % 2], IB * b
        cols = slice(k * NT, (k + 1) * NT)
        mb = jnp.concatenate([m_ref[u % 2]] * LT, axis=1)
        for r in range(0, n, CH):
            es = []
            for r8 in range(r, r + CH, 8):
                pe, t = pen(b, r8, k), (lo + r8) // R
                sub = mb + pe if pe is not None else (mb + tp[t] if t < 4 else mb)
                es.append(jnp.exp2(s[r8 : r8 + 8, cols] * C - sub))
            p[r : r + CH, cols] = jnp.concatenate(es, 0).astype(BF16)

    def pv_all(u):
        hh, x = units[u]
        lo, p = IB * blocks[x], Pm[u % 2]
        o = l = None
        for k in range(KS):
            cols = slice(k * NT, (k + 1) * NT)
            rt = lax.dot_general(
                vt[:, lo : lo + n], p[:, cols], (((1,), (0,)), ((), ())), preferred_element_type=F32
            )
            for t in range(LT):
                part = slice(t * 128, (t + 1) * 128)
                y = rt[0:HS, part] * w2t[x, :, k * NT + t * 128 : k * NT + (t + 1) * 128]
                z = rt[HS : HS + 8, part]
                o, l = (y, z) if o is None else (o + y, l + z)
        l = l[0:1, :]
        l = l + pltpu.roll(l, 32, 1)
        l = l + pltpu.roll(l, 64, 1)
        o = o + pltpu.roll(o, 32, 1)
        o = o + pltpu.roll(o, 64, 1)
        o = (o / l).T
        rows, o = slice(IB * x, IB * (x + 1)), o[0:IB, :].astype(BF16)
        if final:
            att[rows, pl.ds(pl.multiple_of(done_ref.shape[1] + (2 * g + hh) * HS, HS), HS)] = o
        else:
            o_ref[rows, hh * HS : (hh + 1) * HS] = o

    for t in range(-1, len(units) + 1):

        @pl.when(sh >= 0)
        def _():
            if t + 1 < len(units):
                qk_all(t + 1)
            if 0 <= t < len(units):
                for k in range(KS):
                    ex(t, k)
            if t >= 1:
                pv_all(t - 1)

    if not final:
        return

    @pl.when(g == last)
    def _():
        for i in range(4):
            fetch(i).wait()
        width = outs[0].shape[1]
        for d, out in enumerate(outs):
            start = pl.multiple_of(lax.rem(me + d, 4) * width, width)
            out[...] = lax.dot_general(
                att[...], wbuf[:, pl.ds(start, width)], (((1,), (0,)), ((), ())),
                preferred_element_type=F32,
            ).astype(BF16)


def attend(half, shard, me, q, k2, v2, pieces, done=None, weight=None):
    final = weight is not None
    groups = k2.shape[1] // HS // 2
    g0 = half * groups
    nb = R // IB
    kblock = pl.BlockSpec((R, HS), lambda g: (0, g))
    vblock = pl.BlockSpec((R, HS), lambda g: (1, g))
    own = pl.BlockSpec((R, HS), lambda g: (0, g0 + g))
    args = [shard, me, q, k2, v2, pieces[1], pieces[1], pieces[3], pieces[3]]
    for piece in pieces:
        args += [piece, piece]
    specs = [
        pl.BlockSpec(memory_space=pltpu.SMEM),
        pl.BlockSpec(memory_space=pltpu.SMEM),
        pl.BlockSpec((R, 2 * HS), lambda g: (0, g0 + g)),
        own,
        own,
    ]
    specs += [
        pl.BlockSpec((W2, HS), lambda g: (2 * R // W2, g)),
        pl.BlockSpec((W2, HS), lambda g: (2 * R // W2 + 1, g)),
    ] * 2
    specs += [kblock, vblock] * len(pieces)
    scratch = [pltpu.VMEM((KEYS, HS), BF16), pltpu.VMEM((HS + 16, KEYS), BF16)]
    scratch += [pltpu.VMEM((W2 + R, HS), F32)] * 2
    scratch += [pltpu.VMEM((nb, HS, LANES), F32)]
    scratch += [pltpu.VMEM((IB, LANES), F32), pltpu.VMEM((2, IB, LANES), F32)]
    scratch += [pltpu.VMEM((LANES, HS), BF16)] * 2
    scratch += [pltpu.VMEM((W1 + IB, LANES), F32)] * 2
    scratch += [pltpu.VMEM((W1 + IB, LANES), BF16)] * 2
    scratch += [pltpu.VMEM((2, 8, HS), F32)]
    if final:
        width = weight.shape[1] // 4
        out_shape = (jax.ShapeDtypeStruct((R, width), BF16),) * 4
        out_specs = (pl.BlockSpec((R, width), lambda g: (0, 0)),) * 4
        args += [done, weight]
        specs += [pl.BlockSpec(done.shape, lambda g: (0, 0)), pl.BlockSpec(memory_space=pl.ANY)]
        scratch += [pltpu.VMEM(q.shape, BF16), pltpu.VMEM(weight.shape, BF16)]
        scratch += [pltpu.SemaphoreType.DMA((4,))]
    else:
        out_shape = jax.ShapeDtypeStruct((R, 2 * HS * groups), BF16)
        out_specs = pl.BlockSpec((R, 2 * HS), lambda g: (0, g))
    return pl.pallas_call(
        lambda *refs: attn_body(tuple(range(nb)), final, *refs),
        out_shape=out_shape,
        grid=(groups,),
        in_specs=specs,
        out_specs=out_specs,
        scratch_shapes=scratch,
        compiler_params=PARAMS,
        cost_estimate=pl.CostEstimate(
            flops=4 * W2 * R * KEYS * HS * 2 * groups * 4,
            bytes_accessed=12 * 2**20,
            transcendentals=W2 * R * W1 * 2 * groups,
        ),
    )(*args)


def pack_body(k_ref, v_ref, k2_ref, v2_ref, *outs):
    cols = outs[0].shape[1]
    for half in range(2):
        here = slice(half * cols, (half + 1) * cols)
        kv_ref, all_ref = outs[2 * half : 2 * half + 2]
        for ref in (kv_ref, all_ref):
            ref[0:R, :] = k_ref[:, here]
            ref[R : 2 * R, :] = v_ref[:, here]
        all_ref[2 * R : 2 * R + W2, :] = k2_ref[:, here]
        all_ref[2 * R + W2 :, :] = v2_ref[:, here]


def pack(k, v, k2, v2):
    width = k.shape[1]
    cols = width // 2
    block = pl.BlockSpec((R, width), lambda i: (0, 0))
    last = pl.BlockSpec((W2, width), lambda i: (R // W2 - 1, 0))
    shapes = [(2 * R, cols), (2 * R + 2 * W2, cols)] * 2
    return pl.pallas_call(
        pack_body,
        out_shape=tuple(jax.ShapeDtypeStruct(x, BF16) for x in shapes),
        grid=(1,),
        in_specs=[block, block, last, last],
        out_specs=tuple(pl.BlockSpec(x, lambda i: (0, 0)) for x in shapes),
        compiler_params=SMALL,
        name="pack",
    )(k, v, k2, v2)


def add_body(*refs):
    x = [r[...].astype(F32) for r in refs[:-1]]
    refs[-1][...] = (x[0] + x[1] + x[2] + x[3]).astype(BF16)


def local(queries, first_key_rows, first_value_rows, second_key_rows, second_value_rows, out_weight):
    seq = lax.axis_size("seq")
    shard = lax.axis_index("seq").astype(jnp.int32).reshape(1)
    me = lax.axis_index("head").astype(jnp.int32).reshape(1)

    def behind(x, by):
        return lax.ppermute(x, "seq", [(i, (i + by) % seq) for i in range(seq)])

    def swap(x):
        return lax.ppermute(x, "seq", [(i, i ^ 1) for i in range(seq)])

    kva, alla, kvb, allb = pack(
        first_key_rows, first_value_rows, second_key_rows, second_value_rows
    )
    p2a = behind(alla, 2)
    p4a = behind(kva, 4)
    x0a = swap(alla)
    p2a, p4a, sendb, kvsend = lax.optimization_barrier((p2a, p4a, allb, kvb))
    x2a = swap(p2a)
    x4a = swap(p4a)
    p2b = behind(sendb, 2)
    p4b = behind(kvsend, 4)
    x0b = swap(sendb)
    common = (shard, me) + tuple(
        pltpu.with_memory_space_constraint(x, pltpu.HBM)
        for x in (queries, second_key_rows, second_value_rows)
    )
    done = attend(0, *common, (kva, x0a, p2a, x2a, p4a, x4a))
    x2b = swap(p2b)
    x4b = swap(p4b)
    pieces = attend(1, *common, (kvb, x0b, p2b, x2b, p4b, x4b), done, out_weight)
    got = [pieces[0]]
    for d in (2, 1, 3):
        got.append(lax.ppermute(pieces[d], "head", [(i, (i + d) % 4) for i in range(4)]))
    cols = queries.shape[1] // 2
    block = pl.BlockSpec((R, cols), lambda i: (0, i))
    return pl.pallas_call(
        add_body,
        out_shape=jax.ShapeDtypeStruct(queries.shape, BF16),
        grid=(2,),
        in_specs=[block] * 4,
        out_specs=block,
        compiler_params=SMALL,
        name="add",
    )(*got)


def solution(mesh):
    in_specs = (P("seq", "head"),) * 5 + (P("head", None),)
    return jax.shard_map(
        local, mesh=mesh, in_specs=in_specs, out_specs=P("seq", "head"), check_vma=False
    )
```

```python
import math

import jax
import jax.numpy as jnp
from jax import lax
from jax.experimental import pallas as pl
from jax.experimental.pallas import tpu as pltpu
from jax.sharding import PartitionSpec as P


HS = 128
W1 = 512
W2 = 32
R = 128
IB = 32
LANES = W2 * IB
KEYS = W1 + R
NT = 512
KS = LANES // NT
LT = NT // 128
CH = 16
C = math.log2(math.e) / math.sqrt(HS)
BIG = 1e30
F32 = jnp.float32
BF16 = jnp.bfloat16
PARAMS = pltpu.CompilerParams(vmem_limit_bytes=46 * 2**20)
SMALL = pltpu.CompilerParams(vmem_limit_bytes=8 * 2**20)


def attn_body(blocks, final, *refs):
    refs = list(refs)
    sh_ref, me_ref, q_ref, k2o, v2o = (refs.pop(0) for _ in range(5))
    tails = [(refs.pop(0), refs.pop(0)) for _ in range(2)]
    pieces = [(refs.pop(0), refs.pop(0)) for _ in range(6)]
    g, last = pl.program_id(0), pl.num_programs(0) - 1
    if final:
        done_ref, w_hbm = refs.pop(0), refs.pop(0)
        outs = [refs.pop(0) for _ in range(4)]
        att, wbuf, wsem = refs[-3:]
        refs = refs[:-3]
        depth = w_hbm.shape[0] // 4

        def fetch(i):
            rows = slice(i * depth, (i + 1) * depth)
            return pltpu.make_async_copy(w_hbm.at[rows, :], wbuf.at[rows, :], wsem.at[i])

        @pl.when(g == 0)
        def _():
            for i in range(4):
                fetch(i).start()
            att[:, 0 : done_ref.shape[1]] = done_ref[...]

    else:
        o_ref = refs.pop(0)
    ks, vt, k2f, v2f, w2t, penA, penB, a0, a1, s0, s1, p0, p1, m_ref = refs

    sh, me = sh_ref[0], me_ref[0]
    tp = [jnp.where(sh - 4 + t < 0, BIG, 0.0).astype(F32) for t in range(4)]

    def put(tile, piece):
        rows = slice(tile * R, (tile + 1) * R)
        ks[rows, :] = piece[0][...]
        vt[0:HS, rows] = piece[1][...].T

    own, x0, p2, x2, p4, x4 = pieces
    even = lax.rem(sh, 2) == 0
    put(0, p4)
    put(2, p2)

    @pl.when(even)
    def _():
        put(1, x4)
        put(3, x2)
        k2f[0:W2, :] = tails[1][0][...].astype(F32)
        v2f[0:W2, :] = tails[1][1][...].astype(F32)

    @pl.when(jnp.logical_not(even))
    def _():
        put(1, x2)
        put(3, x0)
        k2f[0:W2, :] = tails[0][0][...].astype(F32)
        v2f[0:W2, :] = tails[0][1][...].astype(F32)

    put(4, own)

    @pl.when(pl.program_id(0) == 0)
    def _():
        vt[HS:, :] = jnp.ones((16, KEYS), BF16)
        r = lax.broadcasted_iota(jnp.int32, (IB, LANES), 0)
        lane = lax.broadcasted_iota(jnp.int32, (IB, LANES), 1)
        ii, w = lax.rem(lane, IB), lax.div(lane, IB)
        penA[...] = jnp.where(r > ii, tp[0], BIG)
        penB[0] = jnp.where((r > ii) | ((sh == 0) & (w > ii)), BIG, 0.0)
        penB[1] = jnp.where(r > ii, BIG, 0.0)

    k2f[W2:, :] = k2o[...].astype(F32)
    v2f[W2:, :] = v2o[...].astype(F32)
    for x, b in enumerate(blocks):
        for w in range(0, W2, 4):
            at = W2 + IB * b - w
            blk = jnp.concatenate([v2f[at - y : at - y + IB, :] for y in range(4)], 0)
            w2t[x, :, w * IB : (w + 4) * IB] = blk.T

    A, S, Pm = [a0, a1], [s0, s1], [p0, p1]
    units = [(hh, x) for hh in range(2) for x in range(len(blocks))]
    n = W1 + IB

    def pen(b, r, k):
        cols = slice(k * NT, (k + 1) * NT)
        if r < IB:
            return penA[r : r + 8, cols]
        if r >= W1:
            return penB[0 if b == 0 else 1, r - W1 : r - W1 + 8, cols]
        return None

    def qk(u, k):
        hh, b = units[u][0], blocks[units[u][1]]
        a, s, lo = A[u % 2], S[u % 2], IB * b
        qf = q_ref[lo : lo + IB, hh * HS : (hh + 1) * HS].astype(F32)
        cols = slice(k * NT, (k + 1) * NT)
        for w in range(k * NT // IB, (k + 1) * NT // IB):
            at = W2 + lo - w
            a[w * IB : (w + 1) * IB, :] = (qf * k2f[at : at + IB, :]).astype(BF16)
        x = lax.dot_general(
            ks[lo : lo + n, :], a[cols, :], (((1,), (1,)), ((), ())), preferred_element_type=F32
        )
        s[:, cols] = x
        top = {}
        for r in range(0, n, 8):
            y, pe = x[r : r + 8, :], pen(b, r, k)
            key = "m" if pe is not None else (lo + r) // R
            if pe is not None:
                y = y - pe
            top[key] = y if key not in top else jnp.maximum(top[key], y)
        m8 = None
        for key, y in top.items():
            if key != "m" and key != 4:
                y = y - tp[key]
            for t in range(LT):
                z = y[:, t * 128 : (t + 1) * 128]
                m8 = z if m8 is None else jnp.maximum(m8, z)
        return m8

    def qk_all(u):
        m8 = qk(u, 0)
        for k in range(1, KS):
            m8 = jnp.maximum(m8, qk(u, k))
        m1 = jnp.max(m8, axis=0, keepdims=True)
        m1 = jnp.maximum(m1, pltpu.roll(m1, 32, 1))
        m1 = jnp.maximum(m1, pltpu.roll(m1, 64, 1))
        m_ref[u % 2] = jnp.broadcast_to(m1 * C, (8, HS))

    def ex(u, k):
        b = blocks[units[u][1]]
        s, p, lo = S[u % 2], Pm[u % 2], IB * b
        cols = slice(k * NT, (k + 1) * NT)
        mb = jnp.concatenate([m_ref[u % 2]] * LT, axis=1)
        for r in range(0, n, CH):
            es = []
            for r8 in range(r, r + CH, 8):
                pe, t = pen(b, r8, k), (lo + r8) // R
                sub = mb + pe if pe is not None else (mb + tp[t] if t < 4 else mb)
                es.append(jnp.exp2(s[r8 : r8 + 8, cols] * C - sub))
            p[r : r + CH, cols] = jnp.concatenate(es, 0).astype(BF16)

    def pv_all(u):
        hh, x = units[u]
        lo, p = IB * blocks[x], Pm[u % 2]
        o = l = None
        for k in range(KS):
            cols = slice(k * NT, (k + 1) * NT)
            rt = lax.dot_general(
                vt[:, lo : lo + n], p[:, cols], (((1,), (0,)), ((), ())), preferred_element_type=F32
            )
            for t in range(LT):
                part = slice(t * 128, (t + 1) * 128)
                y = rt[0:HS, part] * w2t[x, :, k * NT + t * 128 : k * NT + (t + 1) * 128]
                z = rt[HS : HS + 8, part]
                o, l = (y, z) if o is None else (o + y, l + z)
        l = l[0:1, :]
        l = l + pltpu.roll(l, 32, 1)
        l = l + pltpu.roll(l, 64, 1)
        o = o + pltpu.roll(o, 32, 1)
        o = o + pltpu.roll(o, 64, 1)
        o = (o / l).T
        rows, o = slice(IB * x, IB * (x + 1)), o[0:IB, :].astype(BF16)
        if final:
            att[rows, pl.ds(pl.multiple_of(done_ref.shape[1] + (2 * g + hh) * HS, HS), HS)] = o
        else:
            o_ref[rows, hh * HS : (hh + 1) * HS] = o

    for t in range(-1, len(units) + 1):

        @pl.when(sh >= 0)
        def _():
            if t + 1 < len(units):
                qk_all(t + 1)
            if 0 <= t < len(units):
                for k in range(KS):
                    ex(t, k)
            if t >= 1:
                pv_all(t - 1)

    if not final:
        return

    @pl.when(g == last)
    def _():
        for i in range(4):
            fetch(i).wait()
        width = outs[0].shape[1]
        for d, out in enumerate(outs):
            start = pl.multiple_of(lax.rem(me + d, 4) * width, width)
            out[...] = lax.dot_general(
                att[...], wbuf[:, pl.ds(start, width)], (((1,), (0,)), ((), ())),
                preferred_element_type=F32,
            ).astype(BF16)


def attend(half, shard, me, q, k2, v2, pieces, done=None, weight=None):
    final = weight is not None
    groups = k2.shape[1] // HS // 2
    g0 = half * groups
    nb = R // IB
    kblock = pl.BlockSpec((R, HS), lambda g: (0, g))
    vblock = pl.BlockSpec((R, HS), lambda g: (1, g))
    own = pl.BlockSpec((R, HS), lambda g: (0, g0 + g))
    args = [shard, me, q, k2, v2, pieces[1], pieces[1], pieces[3], pieces[3]]
    for piece in pieces:
        args += [piece, piece]
    specs = [
        pl.BlockSpec(memory_space=pltpu.SMEM),
        pl.BlockSpec(memory_space=pltpu.SMEM),
        pl.BlockSpec((R, 2 * HS), lambda g: (0, g0 + g)),
        own,
        own,
    ]
    specs += [
        pl.BlockSpec((W2, HS), lambda g: (2 * R // W2, g)),
        pl.BlockSpec((W2, HS), lambda g: (2 * R // W2 + 1, g)),
    ] * 2
    specs += [kblock, vblock] * len(pieces)
    scratch = [pltpu.VMEM((KEYS, HS), BF16), pltpu.VMEM((HS + 16, KEYS), BF16)]
    scratch += [pltpu.VMEM((W2 + R, HS), F32)] * 2
    scratch += [pltpu.VMEM((nb, HS, LANES), F32)]
    scratch += [pltpu.VMEM((IB, LANES), F32), pltpu.VMEM((2, IB, LANES), F32)]
    scratch += [pltpu.VMEM((LANES, HS), BF16)] * 2
    scratch += [pltpu.VMEM((W1 + IB, LANES), F32)] * 2
    scratch += [pltpu.VMEM((W1 + IB, LANES), BF16)] * 2
    scratch += [pltpu.VMEM((2, 8, HS), F32)]
    if final:
        width = weight.shape[1] // 4
        out_shape = (jax.ShapeDtypeStruct((R, width), BF16),) * 4
        out_specs = (pl.BlockSpec((R, width), lambda g: (0, 0)),) * 4
        args += [done, weight]
        specs += [pl.BlockSpec(done.shape, lambda g: (0, 0)), pl.BlockSpec(memory_space=pl.ANY)]
        scratch += [pltpu.VMEM(q.shape, BF16), pltpu.VMEM(weight.shape, BF16)]
        scratch += [pltpu.SemaphoreType.DMA((4,))]
    else:
        out_shape = jax.ShapeDtypeStruct((R, 2 * HS * groups), BF16)
        out_specs = pl.BlockSpec((R, 2 * HS), lambda g: (0, g))
    return pl.pallas_call(
        lambda *refs: attn_body(tuple(range(nb)), final, *refs),
        out_shape=out_shape,
        grid=(groups,),
        in_specs=specs,
        out_specs=out_specs,
        scratch_shapes=scratch,
        compiler_params=PARAMS,
        cost_estimate=pl.CostEstimate(
            flops=4 * W2 * R * KEYS * HS * 2 * groups * 4,
            bytes_accessed=12 * 2**20,
            transcendentals=W2 * R * W1 * 2 * groups,
        ),
    )(*args)


def pack_body(k_ref, v_ref, k2_ref, v2_ref, *outs):
    cols = outs[0].shape[1]
    for half in range(2):
        here = slice(half * cols, (half + 1) * cols)
        kv_ref, all_ref = outs[2 * half : 2 * half + 2]
        for ref in (kv_ref, all_ref):
            ref[0:R, :] = k_ref[:, here]
            ref[R : 2 * R, :] = v_ref[:, here]
        all_ref[2 * R : 2 * R + W2, :] = k2_ref[:, here]
        all_ref[2 * R + W2 :, :] = v2_ref[:, here]


def pack(k, v, k2, v2):
    width = k.shape[1]
    cols = width // 2
    block = pl.BlockSpec((R, width), lambda i: (0, 0))
    last = pl.BlockSpec((W2, width), lambda i: (R // W2 - 1, 0))
    shapes = [(2 * R, cols), (2 * R + 2 * W2, cols)] * 2
    return pl.pallas_call(
        pack_body,
        out_shape=tuple(jax.ShapeDtypeStruct(x, BF16) for x in shapes),
        grid=(1,),
        in_specs=[block, block, last, last],
        out_specs=tuple(pl.BlockSpec(x, lambda i: (0, 0)) for x in shapes),
        compiler_params=SMALL,
        name="pack",
    )(k, v, k2, v2)


def add_body(*refs):
    x = [r[...].astype(F32) for r in refs[:-1]]
    refs[-1][...] = (x[0] + x[1] + x[2] + x[3]).astype(BF16)


def local(queries, first_key_rows, first_value_rows, second_key_rows, second_value_rows, out_weight):
    seq = lax.axis_size("seq")
    shard = lax.axis_index("seq").astype(jnp.int32).reshape(1)
    me = lax.axis_index("head").astype(jnp.int32).reshape(1)

    def behind(x, by):
        return lax.ppermute(x, "seq", [(i, (i + by) % seq) for i in range(seq)])

    def swap(x):
        return lax.ppermute(x, "seq", [(i, i ^ 1) for i in range(seq)])

    queries, first_key_rows, first_value_rows, second_key_rows, second_value_rows = (
        pltpu.with_memory_space_constraint(x, pltpu.HBM)
        for x in (
            queries, first_key_rows, first_value_rows, second_key_rows, second_value_rows
        )
    )
    kva, alla, kvb, allb = pack(
        first_key_rows, first_value_rows, second_key_rows, second_value_rows
    )
    p2a = behind(alla, 2)
    p4a = behind(kva, 4)
    x0a = swap(alla)
    p2a, p4a, sendb, kvsend = lax.optimization_barrier((p2a, p4a, allb, kvb))
    x2a = swap(p2a)
    x4a = swap(p4a)
    p2b = behind(sendb, 2)
    p4b = behind(kvsend, 4)
    x0b = swap(sendb)
    common = (shard, me, queries, second_key_rows, second_value_rows)
    done = attend(0, *common, (kva, x0a, p2a, x2a, p4a, x4a))
    x2b = swap(p2b)
    x4b = swap(p4b)
    pieces = attend(1, *common, (kvb, x0b, p2b, x2b, p4b, x4b), done, out_weight)
    got = [pieces[0]]
    for d in (2, 1, 3):
        got.append(lax.ppermute(pieces[d], "head", [(i, (i + d) % 4) for i in range(4)]))
    cols = queries.shape[1] // 2
    block = pl.BlockSpec((R, cols), lambda i: (0, i))
    return pl.pallas_call(
        add_body,
        out_shape=jax.ShapeDtypeStruct(queries.shape, BF16),
        grid=(2,),
        in_specs=[block] * 4,
        out_specs=block,
        compiler_params=SMALL,
        name="add",
    )(*got)


def solution(mesh):
    in_specs = (P("seq", "head"),) * 5 + (P("head", None),)
    return jax.shard_map(
        local, mesh=mesh, in_specs=in_specs, out_specs=P("seq", "head"), check_vma=False
    )
```

```python
import math

import jax
import jax.numpy as jnp
from jax import lax
from jax.experimental import pallas as pl
from jax.experimental.pallas import tpu as pltpu
from jax.sharding import PartitionSpec as P


HS = 128
W1 = 512
W2 = 32
R = 128
IB = 32
LANES = W2 * IB
KEYS = W1 + R
NT = 512
KS = LANES // NT
LT = NT // 128
CH = 16
C = math.log2(math.e) / math.sqrt(HS)
BIG = 1e30
F32 = jnp.float32
BF16 = jnp.bfloat16
PARAMS = pltpu.CompilerParams(vmem_limit_bytes=46 * 2**20)
SMALL = pltpu.CompilerParams(vmem_limit_bytes=8 * 2**20)


def attn_body(blocks, final, *refs):
    refs = list(refs)
    sh_ref, me_ref, q_ref, k2o, v2o = (refs.pop(0) for _ in range(5))
    tails = [(refs.pop(0), refs.pop(0)) for _ in range(2)]
    pieces = [(refs.pop(0), refs.pop(0)) for _ in range(6)]
    g, last = pl.program_id(0), pl.num_programs(0) - 1
    if final:
        done_ref, w_hbm = refs.pop(0), refs.pop(0)
        outs = [refs.pop(0) for _ in range(4)]
        att, wbuf, wsem = refs[-3:]
        refs = refs[:-3]
        depth = w_hbm.shape[0] // 4

        def fetch(i):
            rows = slice(i * depth, (i + 1) * depth)
            return pltpu.make_async_copy(w_hbm.at[rows, :], wbuf.at[rows, :], wsem.at[i])

        @pl.when(g == 0)
        def _():
            for i in range(4):
                fetch(i).start()
            att[:, 0 : done_ref.shape[1]] = done_ref[...]

    else:
        o_ref = refs.pop(0)
    ks, vt, k2f, v2f, w2t, penA, penB, a0, a1, s0, s1, p0, p1, m_ref = refs

    sh, me = sh_ref[0], me_ref[0]
    tp = [jnp.where(sh - 4 + t < 0, BIG, 0.0).astype(F32) for t in range(4)]

    def put(tile, piece):
        rows = slice(tile * R, (tile + 1) * R)
        ks[rows, :] = piece[0][...]
        vt[0:HS, rows] = piece[1][...].T

    own, x0, p2, x2, p4, x4 = pieces
    even = lax.rem(sh, 2) == 0
    put(0, p4)
    put(2, p2)

    @pl.when(even)
    def _():
        put(1, x4)
        put(3, x2)
        k2f[0:W2, :] = tails[1][0][...].astype(F32)
        v2f[0:W2, :] = tails[1][1][...].astype(F32)

    @pl.when(jnp.logical_not(even))
    def _():
        put(1, x2)
        put(3, x0)
        k2f[0:W2, :] = tails[0][0][...].astype(F32)
        v2f[0:W2, :] = tails[0][1][...].astype(F32)

    put(4, own)

    @pl.when(pl.program_id(0) == 0)
    def _():
        vt[HS:, :] = jnp.ones((16, KEYS), BF16)
        r = lax.broadcasted_iota(jnp.int32, (IB, LANES), 0)
        lane = lax.broadcasted_iota(jnp.int32, (IB, LANES), 1)
        ii, w = lax.rem(lane, IB), lax.div(lane, IB)
        penA[...] = jnp.where(r > ii, tp[0], BIG)
        penB[0] = jnp.where((r > ii) | ((sh == 0) & (w > ii)), BIG, 0.0)
        penB[1] = jnp.where(r > ii, BIG, 0.0)

    k2f[W2:, :] = k2o[...].astype(F32)
    v2f[W2:, :] = v2o[...].astype(F32)
    for x, b in enumerate(blocks):
        for w in range(0, W2, 4):
            at = W2 + IB * b - w
            blk = jnp.concatenate([v2f[at - y : at - y + IB, :] for y in range(4)], 0)
            w2t[x, :, w * IB : (w + 4) * IB] = blk.T

    A, S, Pm = [a0, a1], [s0, s1], [p0, p1]
    units = [(hh, x) for hh in range(2) for x in range(len(blocks))]
    n = W1 + IB

    def pen(b, r, k):
        cols = slice(k * NT, (k + 1) * NT)
        if r < IB:
            return penA[r : r + 8, cols]
        if r >= W1:
            return penB[0 if b == 0 else 1, r - W1 : r - W1 + 8, cols]
        return None

    def qk(u, k):
        hh, b = units[u][0], blocks[units[u][1]]
        a, s, lo = A[u % 2], S[u % 2], IB * b
        qf = q_ref[lo : lo + IB, hh * HS : (hh + 1) * HS].astype(F32)
        cols = slice(k * NT, (k + 1) * NT)
        for w in range(k * NT // IB, (k + 1) * NT // IB):
            at = W2 + lo - w
            a[w * IB : (w + 1) * IB, :] = (qf * k2f[at : at + IB, :]).astype(BF16)
        x = lax.dot_general(
            ks[lo : lo + n, :], a[cols, :], (((1,), (1,)), ((), ())), preferred_element_type=F32
        )
        s[:, cols] = x
        top = {}
        for r in range(0, n, 8):
            y, pe = x[r : r + 8, :], pen(b, r, k)
            key = "m" if pe is not None else (lo + r) // R
            if pe is not None:
                y = y - pe
            top[key] = y if key not in top else jnp.maximum(top[key], y)
        m8 = None
        for key, y in top.items():
            if key != "m" and key != 4:
                y = y - tp[key]
            for t in range(LT):
                z = y[:, t * 128 : (t + 1) * 128]
                m8 = z if m8 is None else jnp.maximum(m8, z)
        return m8

    def qk_all(u):
        m8 = qk(u, 0)
        for k in range(1, KS):
            m8 = jnp.maximum(m8, qk(u, k))
        m1 = jnp.max(m8, axis=0, keepdims=True)
        m1 = jnp.maximum(m1, pltpu.roll(m1, 32, 1))
        m1 = jnp.maximum(m1, pltpu.roll(m1, 64, 1))
        m_ref[u % 2] = jnp.broadcast_to(m1 * C, (8, HS))

    def ex(u, k):
        b = blocks[units[u][1]]
        s, p, lo = S[u % 2], Pm[u % 2], IB * b
        cols = slice(k * NT, (k + 1) * NT)
        mb = jnp.concatenate([m_ref[u % 2]] * LT, axis=1)
        for r in range(0, n, CH):
            es = []
            for r8 in range(r, r + CH, 8):
                pe, t = pen(b, r8, k), (lo + r8) // R
                sub = mb + pe if pe is not None else (mb + tp[t] if t < 4 else mb)
                es.append(jnp.exp2(s[r8 : r8 + 8, cols] * C - sub))
            p[r : r + CH, cols] = jnp.concatenate(es, 0).astype(BF16)

    def pv_all(u):
        hh, x = units[u]
        lo, p = IB * blocks[x], Pm[u % 2]
        o = l = None
        for k in range(KS):
            cols = slice(k * NT, (k + 1) * NT)
            rt = lax.dot_general(
                vt[:, lo : lo + n], p[:, cols], (((1,), (0,)), ((), ())), preferred_element_type=F32
            )
            for t in range(LT):
                part = slice(t * 128, (t + 1) * 128)
                y = rt[0:HS, part] * w2t[x, :, k * NT + t * 128 : k * NT + (t + 1) * 128]
                z = rt[HS : HS + 8, part]
                o, l = (y, z) if o is None else (o + y, l + z)
        l = l[0:1, :]
        l = l + pltpu.roll(l, 32, 1)
        l = l + pltpu.roll(l, 64, 1)
        o = o + pltpu.roll(o, 32, 1)
        o = o + pltpu.roll(o, 64, 1)
        o = (o / l).T
        rows, o = slice(IB * x, IB * (x + 1)), o[0:IB, :].astype(BF16)
        if final:
            att[rows, pl.ds(pl.multiple_of(done_ref.shape[1] + (2 * g + hh) * HS, HS), HS)] = o
        else:
            o_ref[rows, hh * HS : (hh + 1) * HS] = o

    for t in range(-1, len(units) + 1):

        @pl.when(sh >= 0)
        def _():
            if t + 1 < len(units):
                qk_all(t + 1)
            if 0 <= t < len(units):
                for k in range(KS):
                    ex(t, k)
            if t >= 1:
                pv_all(t - 1)

    if not final:
        return

    @pl.when(g == last)
    def _():
        for i in range(4):
            fetch(i).wait()
        width = outs[0].shape[1]
        for d, out in enumerate(outs):
            start = pl.multiple_of(lax.rem(me + d, 4) * width, width)
            out[...] = lax.dot_general(
                att[...], wbuf[:, pl.ds(start, width)], (((1,), (0,)), ((), ())),
                preferred_element_type=F32,
            ).astype(BF16)


def attend(half, part, shard, me, q, k2, v2, pieces, done=None, weight=None):
    final = weight is not None
    groups = k2.shape[1] // HS // 2
    g0 = half * groups
    blocks = tuple(range(R // IB)) if part is None else (2 * part, 2 * part + 1)
    nb = len(blocks)
    rows = nb * IB
    kblock = pl.BlockSpec((R, HS), lambda g: (0, g))
    vblock = pl.BlockSpec((R, HS), lambda g: (1, g))
    own = pl.BlockSpec((R, HS), lambda g: (0, g0 + g))
    args = [shard, me, q, k2, v2, pieces[1], pieces[1], pieces[3], pieces[3]]
    for piece in pieces:
        args += [piece, piece]
    specs = [
        pl.BlockSpec(memory_space=pltpu.SMEM),
        pl.BlockSpec(memory_space=pltpu.SMEM),
        pl.BlockSpec((R, 2 * HS), lambda g: (0, g0 + g)),
        own,
        own,
    ]
    specs += [
        pl.BlockSpec((W2, HS), lambda g: (2 * R // W2, g)),
        pl.BlockSpec((W2, HS), lambda g: (2 * R // W2 + 1, g)),
    ] * 2
    specs += [kblock, vblock] * len(pieces)
    scratch = [pltpu.VMEM((KEYS, HS), BF16), pltpu.VMEM((HS + 16, KEYS), BF16)]
    scratch += [pltpu.VMEM((W2 + R, HS), F32)] * 2
    scratch += [pltpu.VMEM((nb, HS, LANES), F32)]
    scratch += [pltpu.VMEM((IB, LANES), F32), pltpu.VMEM((2, IB, LANES), F32)]
    scratch += [pltpu.VMEM((LANES, HS), BF16)] * 2
    scratch += [pltpu.VMEM((W1 + IB, LANES), F32)] * 2
    scratch += [pltpu.VMEM((W1 + IB, LANES), BF16)] * 2
    scratch += [pltpu.VMEM((2, 8, HS), F32)]
    if final:
        width = weight.shape[1] // 4
        out_shape = (jax.ShapeDtypeStruct((rows, width), BF16),) * 4
        out_specs = (pl.BlockSpec((rows, width), lambda g: (0, 0)),) * 4
        args += [done, weight]
        specs += [
            pl.BlockSpec((rows, done.shape[1]), lambda g: (part, 0)),
            pl.BlockSpec(memory_space=pl.ANY),
        ]
        scratch += [pltpu.VMEM((rows, q.shape[1]), BF16), pltpu.VMEM(weight.shape, BF16)]
        scratch += [pltpu.SemaphoreType.DMA((4,))]
    else:
        out_shape = jax.ShapeDtypeStruct((R, 2 * HS * groups), BF16)
        out_specs = pl.BlockSpec((R, 2 * HS), lambda g: (0, g))
    return pl.pallas_call(
        lambda *refs: attn_body(blocks, final, *refs),
        out_shape=out_shape,
        grid=(groups,),
        in_specs=specs,
        out_specs=out_specs,
        scratch_shapes=scratch,
        compiler_params=PARAMS,
        cost_estimate=pl.CostEstimate(
            flops=4 * W2 * rows * KEYS * HS * 2 * groups * 4,
            bytes_accessed=12 * 2**20,
            transcendentals=W2 * rows * W1 * 2 * groups,
        ),
    )(*args)


def pack_body(k_ref, v_ref, k2_ref, v2_ref, *outs):
    cols = outs[0].shape[1]
    for half in range(2):
        here = slice(half * cols, (half + 1) * cols)
        kv_ref, all_ref = outs[2 * half : 2 * half + 2]
        for ref in (kv_ref, all_ref):
            ref[0:R, :] = k_ref[:, here]
            ref[R : 2 * R, :] = v_ref[:, here]
        all_ref[2 * R : 2 * R + W2, :] = k2_ref[:, here]
        all_ref[2 * R + W2 :, :] = v2_ref[:, here]


def pack(k, v, k2, v2):
    width = k.shape[1]
    cols = width // 2
    block = pl.BlockSpec((R, width), lambda i: (0, 0))
    last = pl.BlockSpec((W2, width), lambda i: (R // W2 - 1, 0))
    shapes = [(2 * R, cols), (2 * R + 2 * W2, cols)] * 2
    return pl.pallas_call(
        pack_body,
        out_shape=tuple(jax.ShapeDtypeStruct(x, BF16) for x in shapes),
        grid=(1,),
        in_specs=[block, block, last, last],
        out_specs=tuple(pl.BlockSpec(x, lambda i: (0, 0)) for x in shapes),
        compiler_params=SMALL,
        name="pack",
    )(k, v, k2, v2)


def add_body(*refs):
    out = refs[-1]
    rows = out.shape[0] // 2
    for part in range(2):
        x = [r[...].astype(F32) for r in refs[4 * part : 4 * part + 4]]
        out[part * rows : (part + 1) * rows, :] = (x[0] + x[1] + x[2] + x[3]).astype(BF16)


def local(queries, first_key_rows, first_value_rows, second_key_rows, second_value_rows, out_weight):
    seq = lax.axis_size("seq")
    shard = lax.axis_index("seq").astype(jnp.int32).reshape(1)
    me = lax.axis_index("head").astype(jnp.int32).reshape(1)

    def behind(x, by):
        return lax.ppermute(x, "seq", [(i, (i + by) % seq) for i in range(seq)])

    def swap(x):
        return lax.ppermute(x, "seq", [(i, i ^ 1) for i in range(seq)])

    queries, first_key_rows, first_value_rows, second_key_rows, second_value_rows = (
        pltpu.with_memory_space_constraint(x, pltpu.HBM)
        for x in (
            queries, first_key_rows, first_value_rows, second_key_rows, second_value_rows
        )
    )
    kva, alla, kvb, allb = pack(
        first_key_rows, first_value_rows, second_key_rows, second_value_rows
    )
    p2a = behind(alla, 2)
    p4a = behind(kva, 4)
    x0a = swap(alla)
    p2a, p4a, sendb, kvsend = lax.optimization_barrier((p2a, p4a, allb, kvb))
    x2a = swap(p2a)
    x4a = swap(p4a)
    p2b = behind(sendb, 2)
    p4b = behind(kvsend, 4)
    x0b = swap(sendb)
    common = (shard, me, queries, second_key_rows, second_value_rows)
    done = attend(0, None, *common, (kva, x0a, p2a, x2a, p4a, x4a))
    x2b = swap(p2b)
    x4b = swap(p4b)
    last = (kvb, x0b, p2b, x2b, p4b, x4b)
    halves = [attend(1, 0, *common, last, done, out_weight)]
    halves.append(attend(1, 1, *common, last, done, out_weight))
    got = []
    for pieces in halves:
        got.append(pieces[0])
        for d in (2, 1, 3):
            got.append(lax.ppermute(pieces[d], "head", [(i, (i + d) % 4) for i in range(4)]))
    return pl.pallas_call(
        add_body,
        out_shape=jax.ShapeDtypeStruct(queries.shape, BF16),
        grid=(1,),
        in_specs=[pl.BlockSpec((R // 2, queries.shape[1]), lambda i: (0, 0))] * 8,
        out_specs=pl.BlockSpec(queries.shape, lambda i: (0, 0)),
        compiler_params=SMALL,
        name="add",
    )(*got)


def solution(mesh):
    in_specs = (P("seq", "head"),) * 5 + (P("head", None),)
    return jax.shard_map(
        local, mesh=mesh, in_specs=in_specs, out_specs=P("seq", "head"), check_vma=False
    )
```
